32 devices in a mesh: prompt: 4 (over z), tensor: 8 (over y, x, core).
Axes of the slice: x: 2, y: 2, z: 4, core: 2. Of those that a mesh axis runs over, the one named last changes fastest.
Arguments:
- embeds: bfloat16 [4, 64, 8192], P('prompt', None, 'tensor'), may hold values from -400 to 400
- norm_gain: bfloat16 [8192], replicated, may hold values from 0.5 to 1.5
- query_weight: bfloat16 [8192, 8192], P('prompt', 'tensor'), may hold values from -1 to 1
- key_weight: bfloat16 [8192, 1024], P('prompt', 'tensor'), may hold values from -6 to 6
- value_weight: bfloat16 [8192, 1024], P('prompt', 'tensor'), may hold values from -0.0625 to 0.0625
- out_weight: bfloat16 [8192, 8192], P('tensor', 'prompt'), may hold values from -0.0625 to 0.0625
- out_grad: bfloat16 [4, 64, 8192], P('prompt', None, 'tensor'), may hold values from -6 to 6
- suffix_pos: int32 [4, 20], P('prompt'), may hold values from 0 to 63
- vocab_table: bfloat16 [65536, 8192], P(('prompt', 'tensor')), may hold values from -0.0625 to 0.0625
- banned: int32 [65536], P(('prompt', 'tensor')), may hold values 0 or 1
Outputs:
- token_scores: float32 [4, 20, 65536], P(None, None, ('prompt', 'tensor'))
The draws below stay inside these ranges and needn't reach their ends.
All inputs are finite; a program needn't handle non-finite values. No bound on the sum of `banned` on one device may be relied on, other than what follows from the above.
Results may differ from the reference program's by a relative error of at most 0.01.
The reference program's roundings to bfloat16 on the way (of `normed`, `probs_low`, `context_grad`, `logit_grad`, `query_grad`, `key_grad`, `value_grad` and `suffix_grad`) count: a program that leaves them out, or rounds other values in their place, can miss the bound.
Values may be sent and summed in bfloat16 or wider, within the bound.
A program may use at most 192 MiB of HBM per device.

```python
import math
import jax
import jax.numpy as jnp
from jax import lax

D = 8192
H = 64
KVH = 8
HD = 128
V = 65536
SEQ = 64
NSUF = 20
PROMPTS = 4


def shared_query(key):
    subkey = jax.random.fold_in(key, 11)
    return jnp.clip(jax.random.normal(subkey, (D, H * HD), jnp.float32), -4.0, 4.0) / math.sqrt(D)


def draw_query_weight(key, part):
    return shared_query(key).astype(jnp.bfloat16)


def draw_key_weight(key, part):
    subkey = jax.random.fold_in(key, 13)
    return (jnp.clip(jax.random.normal(subkey, (D, KVH * HD), jnp.float32), -4.0, 4.0) / math.sqrt(D)).astype(jnp.bfloat16)


def draw_embeds(key, part):
    shape = (PROMPTS, SEQ, D)
    row_key = jax.random.fold_in(key, 21)
    column_key = jax.random.fold_in(key, 22)
    noise_key = jax.random.fold_in(key, 23)
    row_scale = jnp.exp(jax.random.uniform(row_key, (PROMPTS, SEQ, 1), jnp.float32, 0.0, math.log(10.0)))
    column_scale = jnp.exp(jax.random.uniform(column_key, (1, 1, D), jnp.float32, 0.0, math.log(10.0)))
    noise = jnp.clip(jax.random.normal(noise_key, shape, jnp.float32), -4.0, 4.0)
    return (noise * row_scale * column_scale).astype(jnp.bfloat16)


def touch_ends(values, rng, smallest, high):
    dims = values.shape
    index_at = [jax.random.randint(jax.random.fold_in(rng, axis), (), 0, dims[axis]) for axis in range(len(dims))]
    values = values.at[tuple(index_at)].set(smallest)
    longest = dims.index(max(dims))
    index_at[longest] = (index_at[longest] + 1) % dims[longest]
    return values.at[tuple(index_at)].set(high)


def block_scale(stream_key, dims, cuts, smallest, high):
    level = 1.0
    for dim, blocks in cuts:
        draws = jax.random.uniform(jax.random.fold_in(jax.random.fold_in(stream_key, 6), dim), (blocks,), jnp.float32, smallest / len(cuts), high / len(cuts))
        level = level * jnp.repeat(jnp.exp(draws), dims[dim] // blocks).reshape((-1,) + (1,) * (len(dims) - 1 - dim))
    return level


def bell_draw(rng, shape, width, limit, shards=(), dtype=jnp.bfloat16):
    factor_of = block_scale(rng, shape, shards, -0.22, 0.18) if shards else 1.0
    entries = jax.random.normal(rng, shape, jnp.float32) * width * factor_of
    return jnp.minimum(jnp.maximum(entries, -limit), limit).astype(dtype)


def setup_inputs(seed: int = 0) -> dict:
    keys = jax.random.split(jax.random.key(seed), 11)
    embeds = draw_embeds(jax.random.fold_in(keys[10], 71), 0)
    norm_gain = jnp.clip(1.0 + 0.1 * jax.random.normal(keys[1], (D,), jnp.float32), 0.5, 1.5).astype(jnp.bfloat16)
    query_weight = draw_query_weight(jax.random.fold_in(keys[10], 71), 0)
    key_weight = draw_key_weight(jax.random.fold_in(keys[10], 71), 0)
    value_weight = bell_draw(keys[4], (D, KVH * HD), D ** -0.5, 0.0625, ((0, 4), (1, 8)))
    out_weight = bell_draw(keys[5], (H * HD, D), (H * HD) ** -0.5, 0.0625, ((0, 8), (1, 4)))
    out_grad = bell_draw(keys[6], (PROMPTS, SEQ, D), 1.0, 6.0, ((0, 4), (2, 8)))
    suffix_pos = touch_ends(jax.random.randint(keys[7], (PROMPTS, NSUF), 0, SEQ), jax.random.fold_in(keys[7], 1), 0, SEQ - 1).astype(jnp.int32)
    vocab_table = bell_draw(keys[8], (V, D), D ** -0.5, 0.0625, ((0, 32),))
    banned = touch_ends((jax.random.randint(keys[9], (V,), 0, 8) < 1).astype(jnp.int32), jax.random.fold_in(keys[9], 1), 0, 1)
    return {"embeds": embeds, "norm_gain": norm_gain, "query_weight": query_weight, "key_weight": key_weight, "value_weight": value_weight, "out_weight": out_weight, "out_grad": out_grad, "suffix_pos": suffix_pos, "vocab_table": vocab_table, "banned": banned}


EPSILON = 1e-05

def take_one(rows_block, positions):
    return jnp.take(rows_block, positions, axis=0)

def reference(embeds, norm_gain, query_weight, key_weight, value_weight, out_weight, out_grad, suffix_pos, vocab_table, banned):
    prompts = embeds.shape[0]
    picker = jax.vmap(take_one)
    embeds_float = embeds.astype(jnp.float32)
    inverse_norm = lax.rsqrt(lax.optimization_barrier(jnp.mean(embeds_float * embeds_float, axis=-1, keepdims=True)) + EPSILON)
    gain_float = norm_gain.astype(jnp.float32)
    normed = (embeds_float * inverse_norm * gain_float).astype(jnp.bfloat16)
    flat_normed = normed.reshape(prompts * SEQ, D)
    queries = jnp.dot(flat_normed, query_weight, preferred_element_type=jnp.float32).astype(jnp.bfloat16)
    keys_all = jnp.dot(flat_normed, key_weight, preferred_element_type=jnp.float32).astype(jnp.bfloat16)
    values_all = jnp.dot(flat_normed, value_weight, preferred_element_type=jnp.float32).astype(jnp.bfloat16)
    group_size = H // KVH
    query_heads = queries.reshape(prompts, SEQ, H, HD).astype(jnp.float32)
    key_heads = jnp.tile(keys_all.reshape(prompts, SEQ, KVH, HD), (1, 1, group_size, 1)).astype(jnp.float32)
    value_heads = jnp.tile(values_all.reshape(prompts, SEQ, KVH, HD), (1, 1, group_size, 1)).astype(jnp.float32)
    logit_scale = 1.0 / math.sqrt(HD)
    logits = jnp.einsum('pqhd,pkhd->phqk', query_heads, key_heads) * logit_scale
    row_index = lax.broadcasted_iota(jnp.int32, (SEQ, SEQ), 0)
    col_index = lax.broadcasted_iota(jnp.int32, (SEQ, SEQ), 1)
    causal = col_index <= row_index
    largest = lax.optimization_barrier(jnp.max(jnp.where(causal, logits, -1e+30), axis=-1, keepdims=True))
    raised = jnp.where(causal, jnp.exp(logits - largest), 0.0)
    probs_float = raised / lax.optimization_barrier(jnp.sum(raised, axis=-1, keepdims=True))
    probs_low = probs_float.astype(jnp.bfloat16)
    context_grad = jnp.dot(out_grad.reshape(prompts * SEQ, D), out_weight.T, preferred_element_type=jnp.float32).astype(jnp.bfloat16)
    context_heads = context_grad.reshape(prompts, SEQ, H, HD).astype(jnp.float32)
    prob_grad = jnp.einsum('pqhd,pkhd->phqk', context_heads, value_heads)
    logit_grad = (probs_float * (prob_grad - lax.optimization_barrier(jnp.sum(prob_grad * probs_float, axis=-1, keepdims=True))) * logit_scale).astype(jnp.bfloat16)
    logit_float = logit_grad.astype(jnp.float32)
    query_grad = jnp.einsum('phqk,pkhd->pqhd', logit_float, key_heads).astype(jnp.bfloat16).reshape(prompts, SEQ, H * HD)
    key_each = jnp.einsum('phqk,pqhd->pkhd', logit_float, query_heads)
    key_grad = lax.optimization_barrier(jnp.sum(key_each.reshape(prompts, SEQ, group_size, KVH, HD), axis=2)).astype(jnp.bfloat16).reshape(prompts, SEQ, KVH * HD)
    value_each = jnp.einsum('phqk,pqhd->pkhd', probs_low.astype(jnp.float32), context_heads)
    value_grad = lax.optimization_barrier(jnp.sum(value_each.reshape(prompts, SEQ, group_size, KVH, HD), axis=2)).astype(jnp.bfloat16).reshape(prompts, SEQ, KVH * HD)
    query_rows = picker(query_grad, suffix_pos).reshape(prompts * NSUF, H * HD)
    key_rows = picker(key_grad, suffix_pos).reshape(prompts * NSUF, KVH * HD)
    value_rows = picker(value_grad, suffix_pos).reshape(prompts * NSUF, KVH * HD)
    branch = jnp.dot(query_rows, query_weight.T, preferred_element_type=jnp.float32)
    branch = branch + jnp.dot(key_rows, key_weight.T, preferred_element_type=jnp.float32)
    branch = branch + jnp.dot(value_rows, value_weight.T, preferred_element_type=jnp.float32)
    branch = branch.reshape(prompts, NSUF, D)
    embed_rows = picker(embeds_float, suffix_pos)
    norm_rows = picker(inverse_norm, suffix_pos)
    scaled = embed_rows * norm_rows
    weighted = branch * gain_float
    suffix_grad = (norm_rows * (weighted - scaled * lax.optimization_barrier(jnp.mean(weighted * scaled, axis=-1, keepdims=True)))).astype(jnp.bfloat16)
    scores = -jnp.dot(suffix_grad.reshape(prompts * NSUF, D), vocab_table.T, preferred_element_type=jnp.float32)
    scores = scores.reshape(prompts, NSUF, V)
    return jnp.where(banned[None, None, :] == 1, 0.0, scores)
```

```python
import math

import jax
import jax.numpy as jnp
from jax import lax
from jax.sharding import PartitionSpec as P

KVH = 8
HD = 128


EPSILON = 1e-05


def dot_f32(spec, a, b):
    return jnp.einsum(spec, a, b, preferred_element_type=jnp.float32)


def on_device(
    embeds,
    norm_gain,
    query_weight,
    key_weight,
    value_weight,
    out_weight,
    out_grad,
    suffix_pos,
    vocab_table,
    banned,
):
    n_prompt = lax.axis_size("prompt")
    n_tensor = lax.axis_size("tensor")
    here_prompt = lax.axis_index("prompt")
    here_tensor = lax.axis_index("tensor")
    seq_len = embeds.shape[1]
    suffix_count = suffix_pos.shape[1]
    width = embeds.shape[2] * n_tensor
    rows_here, head_cols = query_weight.shape
    key_cols = key_weight.shape[1]
    heads_here = head_cols // HD
    slice_width = rows_here // n_tensor
    logit_scale = 1.0 / math.sqrt(HD)

    suffix_all = lax.all_gather(suffix_pos, "prompt", axis=0, tiled=True)
    both = jnp.concatenate([embeds, out_grad], axis=1)
    both = lax.all_gather(both, "tensor", axis=2, tiled=True)
    own = both[:, :seq_len].astype(jnp.float32)
    inverse_norm = lax.rsqrt(jnp.mean(own * own, axis=-1, keepdims=True) + EPSILON)
    inverse_norm = lax.all_gather(inverse_norm, "prompt", axis=0, tiled=True)
    both = lax.all_to_all(both, "prompt", split_axis=2, concat_axis=0, tiled=True)
    embeds = both[:, :seq_len]
    out_grad = both[:, seq_len:]
    embeds_float = embeds.astype(jnp.float32)
    gain_rows = lax.dynamic_slice_in_dim(norm_gain, here_prompt * rows_here, rows_here, 0)
    gain_rows = gain_rows.astype(jnp.float32)
    normed = (embeds_float * inverse_norm * gain_rows).astype(jnp.bfloat16)

    parts = jnp.concatenate(
        [
            dot_f32("psd,dc->psc", normed, query_weight),
            dot_f32("psd,dc->psc", normed, key_weight),
            dot_f32("psd,dc->psc", normed, value_weight),
            dot_f32("psd,cd->psc", out_grad, out_weight),
        ],
        axis=2,
    )
    whole = lax.psum_scatter(parts, "prompt", scatter_dimension=0, tiled=True)
    whole = whole[0].astype(jnp.bfloat16)
    queries = whole[:, :head_cols].reshape(seq_len, heads_here, HD)
    key_values = whole[:, head_cols : head_cols + 2 * key_cols]
    contexts = whole[:, head_cols + 2 * key_cols :].reshape(seq_len, heads_here, HD)
    key_values = lax.all_gather(key_values, "tensor", axis=0, tiled=False)
    key_values = key_values.reshape(n_tensor, seq_len, 2, key_cols).transpose(2, 1, 0, 3)
    key_values = key_values.reshape(2, seq_len, KVH * HD)
    fold = min(heads_here, KVH)
    first = ((here_tensor * heads_here) % KVH) * HD
    if fold < KVH:
        key_values = lax.dynamic_slice_in_dim(key_values, first, fold * HD, 2)
    key_values = key_values.reshape(2, seq_len, fold, HD)
    if heads_here > fold:
        key_values = jnp.tile(key_values, (1, 1, heads_here // fold, 1))
    keys, values = key_values[0], key_values[1]

    logits = dot_f32("qhd,khd->hqk", queries, keys) * logit_scale
    row_index = lax.broadcasted_iota(jnp.int32, (seq_len, seq_len), 0)
    col_index = lax.broadcasted_iota(jnp.int32, (seq_len, seq_len), 1)
    causal = col_index <= row_index
    largest = jnp.max(jnp.where(causal, logits, -1e30), axis=-1, keepdims=True)
    raised = jnp.where(causal, jnp.exp(logits - largest), 0.0)
    probs = raised / jnp.sum(raised, axis=-1, keepdims=True)
    probs_low = probs.astype(jnp.bfloat16)
    prob_grad = dot_f32("qhd,khd->hqk", contexts, values)
    logit_grad = (
        probs * (prob_grad - jnp.sum(prob_grad * probs, axis=-1, keepdims=True)) * logit_scale
    ).astype(jnp.bfloat16)
    steps_iota = lax.broadcasted_iota(jnp.int32, (suffix_count, seq_len), 1)
    chooser = (steps_iota == suffix_pos[0][:, None]).astype(jnp.bfloat16)
    logit_rows = dot_f32("ns,hsk->hnk", chooser, logit_grad).astype(jnp.bfloat16)
    query_grad = dot_f32("hnk,khd->nhd", logit_rows, keys).astype(jnp.bfloat16)
    query_grad = query_grad.reshape(suffix_count, head_cols)
    logit_cols = dot_f32("hqk,nk->hnq", logit_grad, chooser).astype(jnp.bfloat16)
    prob_cols = dot_f32("hqk,nk->hnq", probs_low, chooser).astype(jnp.bfloat16)
    key_each = dot_f32("hnq,qhd->nhd", logit_cols, queries)
    value_each = dot_f32("hnq,qhd->nhd", prob_cols, contexts)
    slots = jnp.stack([key_each, value_each])
    slots = slots.reshape(2, suffix_count, heads_here // fold, fold * HD).sum(axis=2)
    if fold < KVH:
        slots = lax.dynamic_update_slice_in_dim(
            jnp.zeros((2, suffix_count, KVH * HD), jnp.float32), slots, first, 2
        )
    grads = lax.psum_scatter(slots, "tensor", scatter_dimension=2, tiled=True)
    grads = grads.astype(jnp.bfloat16)
    grads = jnp.concatenate([query_grad, grads[0], grads[1]], axis=1)
    grads = lax.all_gather(grads, "prompt", axis=0, tiled=True)
    branch = dot_f32("nc,dc->nd", grads[:, :head_cols], query_weight)
    branch = branch + dot_f32("nc,dc->nd", grads[:, head_cols : head_cols + key_cols], key_weight)
    branch = branch + dot_f32("nc,dc->nd", grads[:, head_cols + key_cols :], value_weight)
    share = lax.psum_scatter(branch, "tensor", scatter_dimension=1, tiled=True)

    start = here_tensor * slice_width
    embeds_slice = lax.dynamic_slice_in_dim(embeds, start, slice_width, 2)
    steps_iota = lax.broadcasted_iota(jnp.int32, (n_prompt, suffix_count, seq_len), 2)
    chooser_all = steps_iota == suffix_all[:, :, None]
    embed_rows = dot_f32("pns,psd->pnd", chooser_all.astype(jnp.bfloat16), embeds_slice)
    norm_rows = jnp.sum(
        jnp.where(chooser_all, inverse_norm[:, None, :, 0], 0.0), axis=-1, keepdims=True
    )
    scaled = (embed_rows * norm_rows).reshape(n_prompt * suffix_count, slice_width)
    norm_rows = norm_rows.reshape(n_prompt * suffix_count, 1)
    gain_slice = lax.dynamic_slice_in_dim(gain_rows, start, slice_width, 0)
    weighted = share * gain_slice
    inner = jnp.sum(weighted * scaled, axis=-1, keepdims=True)
    inner = lax.psum(inner, ("prompt", "tensor")) / width
    suffix_grad = (norm_rows * (weighted - scaled * inner)).astype(jnp.bfloat16)
    flat_grads = lax.all_gather(suffix_grad, ("prompt", "tensor"), axis=1, tiled=True)
    scores = -dot_f32("rd,vd->rv", flat_grads, vocab_table)
    scores = scores.reshape(n_prompt, suffix_count, vocab_table.shape[0])
    return jnp.where(banned[None, None, :] == 1, 0.0, scores)


def solution(mesh):
    return jax.shard_map(
        on_device,
        mesh=mesh,
        in_specs=(
            P("prompt", None, "tensor"),
            P(),
            P("prompt", "tensor"),
            P("prompt", "tensor"),
            P("prompt", "tensor"),
            P("tensor", "prompt"),
            P("prompt", None, "tensor"),
            P("prompt", None),
            P(("prompt", "tensor"), None),
            P(("prompt", "tensor")),
        ),
        out_specs=P(None, None, ("prompt", "tensor")),
        check_vma=False,
    )
```

```python
import functools
import math

import jax
import jax.numpy as jnp
from jax import lax
from jax.experimental import pallas as pl
from jax.experimental.pallas import tpu as pltpu
from jax.sharding import PartitionSpec as P

KVH = 8
HD = 128


EPSILON = 1e-05


def exchange_kernel(axis, count, spread, *refs):
    arrays = len(spread)
    sources, targets = refs[:arrays], refs[arrays : 2 * arrays]
    send_sem, recv_sem, own_sem = refs[2 * arrays :]
    here = lax.axis_index(axis)

    def block(i, to):
        return sources[i].at[to] if spread[i] else sources[i]

    kept = []
    for i in range(arrays):
        copy = pltpu.make_async_copy(block(i, here), targets[i].at[here], own_sem.at[i])
        copy.start()
        kept.append(copy)
    barrier = pltpu.get_barrier_semaphore()
    for step in range(1, count):
        peer = lax.rem(here + step, count)
        pl.semaphore_signal(
            barrier, inc=1, device_id={axis: peer}, device_id_type=pl.DeviceIdType.MESH
        )
    pl.semaphore_wait(barrier, count - 1)
    copies = []
    for step in range(1, count):
        peer = lax.rem(here + step, count)
        for i in range(arrays):
            copy = pltpu.make_async_remote_copy(
                src_ref=block(i, peer),
                dst_ref=targets[i].at[here],
                send_sem=send_sem.at[i, step - 1],
                recv_sem=recv_sem.at[i, step - 1],
                device_id={axis: peer},
                device_id_type=pl.DeviceIdType.MESH,
            )
            copy.start()
            copies.append(copy)
    for copy in kept + copies:
        copy.wait()


def exchange(axis, number, *operands):
    count = lax.axis_size(axis)
    arrays = [array for array, _ in operands]
    spread = tuple(each for _, each in operands)
    shapes = [
        jax.ShapeDtypeStruct(((count,) + (a.shape[1:] if each else a.shape)), a.dtype)
        for a, each in operands
    ]
    space = pl.BlockSpec(memory_space=pltpu.VMEM)
    sems = pltpu.SemaphoreType.DMA((len(arrays), count - 1))
    return pl.pallas_call(
        functools.partial(exchange_kernel, axis, count, spread),
        out_shape=shapes,
        in_specs=[space] * len(arrays),
        out_specs=[space] * len(arrays),
        scratch_shapes=[sems, sems, pltpu.SemaphoreType.DMA((len(arrays),))],
        compiler_params=pltpu.CompilerParams(
            collective_id=number, has_side_effects=True, vmem_limit_bytes=40 << 20
        ),
    )(*arrays)


def dot_f32(spec, a, b):
    return jnp.einsum(spec, a, b, preferred_element_type=jnp.float32)


def on_device(
    embeds,
    norm_gain,
    query_weight,
    key_weight,
    value_weight,
    out_weight,
    out_grad,
    suffix_pos,
    vocab_table,
    banned,
):
    n_prompt = lax.axis_size("prompt")
    n_tensor = lax.axis_size("tensor")
    here_prompt = lax.axis_index("prompt")
    here_tensor = lax.axis_index("tensor")
    seq_len = embeds.shape[1]
    suffix_count = suffix_pos.shape[1]
    width = embeds.shape[2] * n_tensor
    rows_here, head_cols = query_weight.shape
    key_cols = key_weight.shape[1]
    heads_here = head_cols // HD
    slice_width = rows_here // n_tensor
    logit_scale = 1.0 / math.sqrt(HD)

    split_rows = seq_len // n_tensor
    ratio = n_tensor // n_prompt
    feature_cols = embeds.shape[2]
    both = jnp.concatenate(
        [
            embeds.reshape(n_tensor, split_rows, feature_cols),
            out_grad.reshape(n_tensor, split_rows, feature_cols),
        ],
        axis=1,
    )
    (both,) = exchange("tensor", 0, (both, True))
    own = both[:, :split_rows].astype(jnp.float32)
    inverse_norm = lax.rsqrt(jnp.sum(own * own, axis=(0, 2))[:, None] / width + EPSILON)
    inverse_norm = jnp.broadcast_to(inverse_norm, (split_rows, 128))
    both = both.reshape(n_prompt, ratio, 2 * split_rows, feature_cols)
    both, inverse_norm, suffix_all = exchange(
        "prompt", 1, (both, True), (inverse_norm, False), (suffix_pos, False)
    )
    both, inverse_norm = exchange("tensor", 2, (both, False), (inverse_norm, False))
    suffix_all = suffix_all.reshape(n_prompt, suffix_count)
    both = both.reshape(n_tensor, n_prompt, ratio, 2, split_rows, feature_cols)
    both = both.transpose(3, 1, 0, 4, 2, 5).reshape(2, n_prompt, seq_len, rows_here)
    embeds, out_grad = both[0], both[1]
    inverse_norm = inverse_norm[..., :1].transpose(1, 0, 2, 3).reshape(n_prompt, seq_len, 1)
    embeds_float = embeds.astype(jnp.float32)
    gain_rows = lax.dynamic_slice_in_dim(norm_gain, here_prompt * rows_here, rows_here, 0)
    gain_rows = gain_rows.astype(jnp.float32)
    normed = (embeds_float * inverse_norm * gain_rows).astype(jnp.bfloat16)

    parts = jnp.concatenate(
        [
            dot_f32("psd,dc->psc", normed, query_weight),
            dot_f32("psd,dc->psc", normed, key_weight),
            dot_f32("psd,dc->psc", normed, value_weight),
        ],
        axis=2,
    )
    context_parts = dot_f32("psd,cd->psc", out_grad, out_weight).astype(jnp.bfloat16)
    parts, context_parts = exchange("prompt", 3, (parts, True), (context_parts, True))
    whole = jnp.sum(parts, axis=0).astype(jnp.bfloat16)
    contexts = jnp.sum(context_parts.astype(jnp.float32), axis=0).astype(jnp.bfloat16)
    contexts = contexts.reshape(seq_len, heads_here, HD)
    queries = whole[:, :head_cols].reshape(seq_len, heads_here, HD)
    (key_values,) = exchange("tensor", 4, (whole[:, head_cols:], False))
    key_values = key_values.reshape(n_tensor, seq_len, 2, key_cols).transpose(2, 1, 0, 3)
    key_values = key_values.reshape(2, seq_len, KVH * HD)
    fold = min(heads_here, KVH)
    first = ((here_tensor * heads_here) % KVH) * HD
    if fold < KVH:
        key_values = lax.dynamic_slice_in_dim(key_values, first, fold * HD, 2)
    key_values = key_values.reshape(2, seq_len, fold, HD)
    if heads_here > fold:
        key_values = jnp.tile(key_values, (1, 1, heads_here // fold, 1))
    keys, values = key_values[0], key_values[1]

    logits = dot_f32("qhd,khd->hqk", queries, keys) * logit_scale
    row_index = lax.broadcasted_iota(jnp.int32, (seq_len, seq_len), 0)
    col_index = lax.broadcasted_iota(jnp.int32, (seq_len, seq_len), 1)
    causal = col_index <= row_index
    largest = jnp.max(jnp.where(causal, logits, -1e30), axis=-1, keepdims=True)
    raised = jnp.where(causal, jnp.exp(logits - largest), 0.0)
    probs = raised / jnp.sum(raised, axis=-1, keepdims=True)
    probs_low = probs.astype(jnp.bfloat16)
    prob_grad = dot_f32("qhd,khd->hqk", contexts, values)
    logit_grad = (
        probs * (prob_grad - jnp.sum(prob_grad * probs, axis=-1, keepdims=True)) * logit_scale
    ).astype(jnp.bfloat16)
    steps_iota = lax.broadcasted_iota(jnp.int32, (suffix_count, seq_len), 1)
    chooser = (steps_iota == suffix_pos[0][:, None]).astype(jnp.bfloat16)
    logit_rows = dot_f32("ns,hsk->hnk", chooser, logit_grad).astype(jnp.bfloat16)
    query_grad = dot_f32("hnk,khd->nhd", logit_rows, keys).astype(jnp.bfloat16)
    query_grad = query_grad.reshape(suffix_count, head_cols)
    logit_cols = dot_f32("hqk,nk->hnq", logit_grad, chooser).astype(jnp.bfloat16)
    prob_cols = dot_f32("hqk,nk->hnq", probs_low, chooser).astype(jnp.bfloat16)
    key_each = dot_f32("hnq,qhd->nhd", logit_cols, queries)
    value_each = dot_f32("hnq,qhd->nhd", prob_cols, contexts)
    slots = jnp.stack([key_each, value_each])
    slots = slots.reshape(2, suffix_count, heads_here // fold, fold * HD).sum(axis=2)
    if fold < KVH:
        slots = lax.dynamic_update_slice_in_dim(
            jnp.zeros((2, suffix_count, KVH * HD), jnp.float32), slots, first, 2
        )
    slots = slots.reshape(2 * suffix_count, n_tensor, key_cols).transpose(1, 0, 2)
    (grads,) = exchange("tensor", 5, (slots, True))
    grads = jnp.sum(grads, axis=0).astype(jnp.bfloat16).reshape(2, suffix_count, key_cols)
    grads = jnp.concatenate([query_grad, grads[0], grads[1]], axis=1)
    (grads,) = exchange("prompt", 6, (grads, False))
    rows = n_prompt * suffix_count
    grads = grads.reshape(rows, head_cols + 2 * key_cols)
    steps_iota = lax.broadcasted_iota(jnp.int32, (n_prompt, suffix_count, seq_len), 2)
    chooser_all = steps_iota == suffix_all[:, :, None]
    embed_rows = dot_f32("pns,psd->pnd", chooser_all.astype(jnp.bfloat16), embeds)
    norm_rows = jnp.sum(
        jnp.where(chooser_all, inverse_norm[:, None, :, 0], 0.0), axis=-1, keepdims=True
    )
    scaled = (embed_rows * norm_rows).reshape(rows, rows_here)
    norm_rows = norm_rows.reshape(rows, 1)
    branch = dot_f32("nc,dc->nd", grads[:, :head_cols], query_weight)
    branch = branch + dot_f32("nc,dc->nd", grads[:, head_cols : head_cols + key_cols], key_weight)
    branch = branch + dot_f32("nc,dc->nd", grads[:, head_cols + key_cols :], value_weight)
    branch = branch * gain_rows
    inner = jnp.sum(branch * scaled, axis=-1)
    branch = branch.reshape(rows, n_tensor, slice_width).transpose(1, 0, 2)
    share, inner = exchange("tensor", 7, (branch, True), (inner[None, :], False))
    weighted = jnp.sum(share, axis=0)
    (inner,) = exchange("prompt", 8, (jnp.sum(inner, axis=0), False))
    inner = jnp.sum(inner, axis=0).reshape(rows, 1) / width
    scaled = lax.dynamic_slice_in_dim(scaled, here_tensor * slice_width, slice_width, 1)
    suffix_grad = (norm_rows * (weighted - scaled * inner)).astype(jnp.bfloat16)
    (suffix_grad,) = exchange("prompt", 9, (suffix_grad, False))
    (suffix_grad,) = exchange("tensor", 10, (suffix_grad, False))
    flat_grads = suffix_grad.transpose(2, 1, 0, 3).reshape(rows, width)
    scores = -dot_f32("rd,vd->rv", flat_grads, vocab_table)
    scores = scores.reshape(n_prompt, suffix_count, vocab_table.shape[0])
    return jnp.where(banned[None, None, :] == 1, 0.0, scores)


def solution(mesh):
    return jax.shard_map(
        on_device,
        mesh=mesh,
        in_specs=(
            P("prompt", None, "tensor"),
            P(),
            P("prompt", "tensor"),
            P("prompt", "tensor"),
            P("prompt", "tensor"),
            P("tensor", "prompt"),
            P("prompt", None, "tensor"),
            P("prompt", None),
            P(("prompt", "tensor"), None),
            P(("prompt", "tensor")),
        ),
        out_specs=P(None, None, ("prompt", "tensor")),
        check_vma=False,
    )
```

```python
import functools
import math

import jax
import jax.numpy as jnp
from jax import lax
from jax.experimental import pallas as pl
from jax.experimental.pallas import tpu as pltpu
from jax.sharding import PartitionSpec as P

KVH = 8
HD = 128


EPSILON = 1e-05


def exchange_kernel(axis, count, spread, *refs):
    arrays = len(spread)
    sources, targets = refs[:arrays], refs[arrays : 2 * arrays]
    send_sem, recv_sem, own_sem = refs[2 * arrays :]
    here = lax.axis_index(axis)

    def block(i, to):
        return sources[i].at[to] if spread[i] else sources[i]

    kept = []
    for i in range(arrays):
        copy = pltpu.make_async_copy(block(i, here), targets[i].at[here], own_sem.at[i])
        copy.start()
        kept.append(copy)
    barrier = pltpu.get_barrier_semaphore()
    for step in range(1, count):
        peer = lax.rem(here + step, count)
        pl.semaphore_signal(
            barrier, inc=1, device_id={axis: peer}, device_id_type=pl.DeviceIdType.MESH
        )
    pl.semaphore_wait(barrier, count - 1)
    copies = []
    for step in range(1, count):
        peer = lax.rem(here + step, count)
        for i in range(arrays):
            copy = pltpu.make_async_remote_copy(
                src_ref=block(i, peer),
                dst_ref=targets[i].at[here],
                send_sem=send_sem.at[i, step - 1],
                recv_sem=recv_sem.at[i, step - 1],
                device_id={axis: peer},
                device_id_type=pl.DeviceIdType.MESH,
            )
            copy.start()
            copies.append(copy)
    for copy in kept + copies:
        copy.wait()


def exchange(axis, number, *operands):
    count = lax.axis_size(axis)
    arrays = [array for array, _ in operands]
    spread = tuple(each for _, each in operands)
    shapes = [
        jax.ShapeDtypeStruct(((count,) + (a.shape[1:] if each else a.shape)), a.dtype)
        for a, each in operands
    ]
    space = pl.BlockSpec(memory_space=pltpu.VMEM)
    sems = pltpu.SemaphoreType.DMA((len(arrays), count - 1))
    return pl.pallas_call(
        functools.partial(exchange_kernel, axis, count, spread),
        out_shape=shapes,
        in_specs=[space] * len(arrays),
        out_specs=[space] * len(arrays),
        scratch_shapes=[sems, sems, pltpu.SemaphoreType.DMA((len(arrays),))],
        compiler_params=pltpu.CompilerParams(
            collective_id=number, has_side_effects=True, vmem_limit_bytes=40 << 20
        ),
    )(*arrays)


def dot_f32(spec, a, b):
    return jnp.einsum(spec, a, b, preferred_element_type=jnp.float32)


MESH = pl.DeviceIdType.MESH


def greet(axis, peers):
    barrier = pltpu.get_barrier_semaphore()
    for peer in peers:
        pl.semaphore_signal(barrier, inc=1, device_id={axis: peer}, device_id_type=MESH)
    pl.semaphore_wait(barrier, len(peers))


def gather_kernel(axis, count, arrays, *refs):
    sources, targets = refs[:arrays], refs[arrays : 2 * arrays]
    send_sem, recv_sem, own_sem = refs[2 * arrays :]
    here = lax.axis_index(axis)
    chips = count // 2
    chip, core = here // 2, lax.rem(here, 2)
    pair = 2 * chip + (1 - core)
    kept = []
    for i in range(arrays):
        copy = pltpu.make_async_copy(sources[i], targets[i].at[here], own_sem.at[i])
        copy.start()
        kept.append(copy)

    def push(i, source, slot, number, peer):
        return pltpu.make_async_remote_copy(
            src_ref=source,
            dst_ref=targets[i].at[slot],
            send_sem=send_sem.at[i, number],
            recv_sem=recv_sem.at[i, number],
            device_id={axis: peer},
            device_id_type=MESH,
        )

    others = [2 * lax.rem(chip + step, chips) + core for step in range(1, chips)]
    greet(axis, others + [pair])
    first = []
    for step in range(1, chips):
        for i in range(arrays):
            copy = push(i, sources[i], here, step, others[step - 1])
            copy.start()
            first.append(copy)
    rest = []
    for i in range(arrays):
        copy = push(i, sources[i], here, 0, pair)
        copy.start()
        rest.append(copy)
    for step in range(1, chips):
        slot = 2 * lax.rem(chip + chips - step, chips) + core
        for i in range(arrays):
            first[(step - 1) * arrays + i].wait_recv()
            copy = push(i, targets[i].at[slot], slot, chips - 1 + step, pair)
            copy.start()
            rest.append(copy)
    for copy in first:
        copy.wait_send()
    for copy in kept + rest:
        copy.wait()


def gather(axis, number, *arrays):
    count = lax.axis_size(axis)
    shapes = [jax.ShapeDtypeStruct((count,) + a.shape, a.dtype) for a in arrays]
    space = pl.BlockSpec(memory_space=pltpu.VMEM)
    sems = pltpu.SemaphoreType.DMA((len(arrays), count - 1))
    return pl.pallas_call(
        functools.partial(gather_kernel, axis, count, len(arrays)),
        out_shape=shapes,
        in_specs=[space] * len(arrays),
        out_specs=[space] * len(arrays),
        scratch_shapes=[sems, sems, pltpu.SemaphoreType.DMA((len(arrays),))],
        compiler_params=pltpu.CompilerParams(
            collective_id=number, has_side_effects=True, vmem_limit_bytes=40 << 20
        ),
    )(*arrays)


def line_kernel(axis, source, target, relay, send_sem, recv_sem, own_sem):
    here = lax.axis_index(axis)
    own = pltpu.make_async_copy(source.at[here], target.at[here], own_sem.at[0])
    own.start()
    greet(axis, [lax.rem(here + step, 4) for step in range(1, 4)])

    def push(block, slot, number, peer, into=None):
        return pltpu.make_async_remote_copy(
            src_ref=block,
            dst_ref=target.at[slot] if into is None else into,
            send_sem=send_sem.at[number],
            recv_sem=recv_sem.at[slot if into is None else 4],
            device_id={axis: peer},
            device_id_type=MESH,
        )

    for role in range(4):
        far = 3 if role < 2 else 0
        middle = 1 if role < 2 else 2
        across = 3 - middle

        @pl.when(here == role)
        def _():
            if role == middle:
                sent = [
                    push(source.at[across], role, 0, across),
                    push(source.at[3 - far], role, 1, 3 - far),
                ]
                for copy in sent:
                    copy.start()
                total = push(relay, role, 2, far)
                push(source.at[far], role, 3, far, relay).wait_recv()
                relay[...] = relay[...] + source[far]
                total.start()
                sent.append(total)
                arriving = [0, across, 3]
            else:
                handed = push(source.at[far], role, 0, middle, relay)
                handed.start()
                target[far] = jnp.zeros_like(target[far])
                handed.wait_send()
                sent = [
                    push(source.at[across], role, 1, across),
                    push(source.at[middle], role, 2, middle),
                ]
                for copy in sent:
                    copy.start()
                arriving = [1, 2]
            for slot in arriving:
                push(source.at[slot], slot, 3, slot).wait_recv()
            for copy in sent:
                copy.wait_send()

    own.wait()


def line_exchange(axis, number, blocks):
    if lax.axis_size(axis) != 4:
        return exchange(axis, number, (blocks, True))[0]
    space = pl.BlockSpec(memory_space=pltpu.VMEM)
    return pl.pallas_call(
        functools.partial(line_kernel, axis),
        out_shape=jax.ShapeDtypeStruct(blocks.shape, blocks.dtype),
        in_specs=[space],
        out_specs=space,
        scratch_shapes=[
            pltpu.VMEM(blocks.shape[1:], blocks.dtype),
            pltpu.SemaphoreType.DMA((4,)),
            pltpu.SemaphoreType.DMA((5,)),
            pltpu.SemaphoreType.DMA((1,)),
        ],
        compiler_params=pltpu.CompilerParams(
            collective_id=number, has_side_effects=True, vmem_limit_bytes=40 << 20
        ),
    )(blocks)


def on_device(
    embeds,
    norm_gain,
    query_weight,
    key_weight,
    value_weight,
    out_weight,
    out_grad,
    suffix_pos,
    vocab_table,
    banned,
):
    n_prompt = lax.axis_size("prompt")
    n_tensor = lax.axis_size("tensor")
    here_prompt = lax.axis_index("prompt")
    here_tensor = lax.axis_index("tensor")
    seq_len = embeds.shape[1]
    suffix_count = suffix_pos.shape[1]
    width = embeds.shape[2] * n_tensor
    rows_here, head_cols = query_weight.shape
    key_cols = key_weight.shape[1]
    heads_here = head_cols // HD
    slice_width = rows_here // n_tensor
    logit_scale = 1.0 / math.sqrt(HD)

    split_rows = seq_len // n_tensor
    ratio = n_tensor // n_prompt
    feature_cols = embeds.shape[2]
    both = jnp.concatenate(
        [
            embeds.reshape(n_tensor, split_rows, feature_cols),
            out_grad.reshape(n_tensor, split_rows, feature_cols),
        ],
        axis=1,
    )
    (both,) = exchange("tensor", 0, (both, True))
    own = both[:, :split_rows].astype(jnp.float32)
    inverse_norm = lax.rsqrt(jnp.sum(own * own, axis=(0, 2))[:, None] / width + EPSILON)
    inverse_norm = jnp.broadcast_to(inverse_norm, (split_rows, 128))
    both = both.reshape(n_prompt, ratio, 2 * split_rows, feature_cols)
    both, inverse_norm, suffix_all = exchange(
        "prompt", 1, (both, True), (inverse_norm, False), (suffix_pos, False)
    )
    both, inverse_norm = gather("tensor", 2, both, inverse_norm)
    suffix_all = suffix_all.reshape(n_prompt, suffix_count)
    both = both.reshape(n_tensor, n_prompt, ratio, 2, split_rows, feature_cols)
    both = both.transpose(3, 1, 0, 4, 2, 5).reshape(2, n_prompt, seq_len, rows_here)
    embeds, out_grad = both[0], both[1]
    inverse_norm = inverse_norm[..., :1].transpose(1, 0, 2, 3).reshape(n_prompt, seq_len, 1)
    embeds_float = embeds.astype(jnp.float32)
    gain_rows = lax.dynamic_slice_in_dim(norm_gain, here_prompt * rows_here, rows_here, 0)
    gain_rows = gain_rows.astype(jnp.float32)
    normed = (embeds_float * inverse_norm * gain_rows).astype(jnp.bfloat16)

    parts = jnp.concatenate(
        [
            dot_f32("psd,dc->psc", normed, query_weight),
            dot_f32("psd,dc->psc", normed, key_weight),
            dot_f32("psd,dc->psc", normed, value_weight),
            dot_f32("psd,cd->psc", out_grad, out_weight),
        ],
        axis=2,
    )
    parts = line_exchange("prompt", 3, parts)
    whole = jnp.sum(parts, axis=0).astype(jnp.bfloat16)
    contexts = whole[:, head_cols + 2 * key_cols :]
    contexts = contexts.reshape(seq_len, heads_here, HD)
    queries = whole[:, :head_cols].reshape(seq_len, heads_here, HD)
    (key_values,) = gather("tensor", 4, whole[:, head_cols : head_cols + 2 * key_cols])
    key_values = key_values.reshape(n_tensor, seq_len, 2, key_cols).transpose(2, 1, 0, 3)
    key_values = key_values.reshape(2, seq_len, KVH * HD)
    fold = min(heads_here, KVH)
    first = ((here_tensor * heads_here) % KVH) * HD
    if fold < KVH:
        key_values = lax.dynamic_slice_in_dim(key_values, first, fold * HD, 2)
    key_values = key_values.reshape(2, seq_len, fold, HD)
    if heads_here > fold:
        key_values = jnp.tile(key_values, (1, 1, heads_here // fold, 1))
    keys, values = key_values[0], key_values[1]

    logits = dot_f32("qhd,khd->hqk", queries, keys) * logit_scale
    row_index = lax.broadcasted_iota(jnp.int32, (seq_len, seq_len), 0)
    col_index = lax.broadcasted_iota(jnp.int32, (seq_len, seq_len), 1)
    causal = col_index <= row_index
    largest = jnp.max(jnp.where(causal, logits, -1e30), axis=-1, keepdims=True)
    raised = jnp.where(causal, jnp.exp(logits - largest), 0.0)
    probs = raised / jnp.sum(raised, axis=-1, keepdims=True)
    probs_low = probs.astype(jnp.bfloat16)
    prob_grad = dot_f32("qhd,khd->hqk", contexts, values)
    logit_grad = (
        probs * (prob_grad - jnp.sum(prob_grad * probs, axis=-1, keepdims=True)) * logit_scale
    ).astype(jnp.bfloat16)
    steps_iota = lax.broadcasted_iota(jnp.int32, (suffix_count, seq_len), 1)
    chooser = (steps_iota == suffix_pos[0][:, None]).astype(jnp.bfloat16)
    logit_rows = dot_f32("ns,hsk->hnk", chooser, logit_grad).astype(jnp.bfloat16)
    query_grad = dot_f32("hnk,khd->nhd", logit_rows, keys).astype(jnp.bfloat16)
    query_grad = query_grad.reshape(suffix_count, head_cols)
    logit_cols = dot_f32("hqk,nk->hnq", logit_grad, chooser).astype(jnp.bfloat16)
    prob_cols = dot_f32("hqk,nk->hnq", probs_low, chooser).astype(jnp.bfloat16)
    key_each = dot_f32("hnq,qhd->nhd", logit_cols, queries)
    value_each = dot_f32("hnq,qhd->nhd", prob_cols, contexts)
    slots = jnp.stack([key_each, value_each])
    slots = slots.reshape(2, suffix_count, heads_here // fold, fold * HD).sum(axis=2)
    if fold < KVH:
        slots = lax.dynamic_update_slice_in_dim(
            jnp.zeros((2, suffix_count, KVH * HD), jnp.float32), slots, first, 2
        )
    slots = slots.reshape(2 * suffix_count, n_tensor, key_cols).transpose(1, 0, 2)
    (grads,) = exchange("tensor", 5, (slots, True))
    grads = jnp.sum(grads, axis=0).astype(jnp.bfloat16).reshape(2, suffix_count, key_cols)
    grads = jnp.concatenate([query_grad, grads[0], grads[1]], axis=1)
    (grads,) = exchange("prompt", 6, (grads, False))
    rows = n_prompt * suffix_count
    grads = grads.reshape(rows, head_cols + 2 * key_cols)
    steps_iota = lax.broadcasted_iota(jnp.int32, (n_prompt, suffix_count, seq_len), 2)
    chooser_all = steps_iota == suffix_all[:, :, None]
    embed_rows = dot_f32("pns,psd->pnd", chooser_all.astype(jnp.bfloat16), embeds)
    norm_rows = jnp.sum(
        jnp.where(chooser_all, inverse_norm[:, None, :, 0], 0.0), axis=-1, keepdims=True
    )
    scaled = (embed_rows * norm_rows).reshape(rows, rows_here)
    norm_rows = norm_rows.reshape(rows, 1)
    branch = dot_f32("nc,dc->nd", grads[:, :head_cols], query_weight)
    branch = branch + dot_f32("nc,dc->nd", grads[:, head_cols : head_cols + key_cols], key_weight)
    branch = branch + dot_f32("nc,dc->nd", grads[:, head_cols + key_cols :], value_weight)
    branch = branch * gain_rows
    inner = jnp.sum(branch * scaled, axis=-1)
    branch = branch.reshape(rows, n_tensor, slice_width).transpose(1, 0, 2)
    share, inner = exchange("tensor", 7, (branch, True), (inner[None, :], False))
    weighted = jnp.sum(share, axis=0)
    (inner,) = exchange("prompt", 8, (jnp.sum(inner, axis=0), False))
    inner = jnp.sum(inner, axis=0).reshape(rows, 1) / width
    scaled = lax.dynamic_slice_in_dim(scaled, here_tensor * slice_width, slice_width, 1)
    suffix_grad = (norm_rows * (weighted - scaled * inner)).astype(jnp.bfloat16)
    (suffix_grad,) = exchange("prompt", 9, (suffix_grad, False))
    (suffix_grad,) = gather("tensor", 10, suffix_grad)
    flat_grads = suffix_grad.transpose(2, 1, 0, 3).reshape(rows, width)
    scores = -dot_f32("rd,vd->rv", flat_grads, vocab_table)
    scores = scores.reshape(n_prompt, suffix_count, vocab_table.shape[0])
    return jnp.where(banned[None, None, :] == 1, 0.0, scores)


def solution(mesh):
    return jax.shard_map(
        on_device,
        mesh=mesh,
        in_specs=(
            P("prompt", None, "tensor"),
            P(),
            P("prompt", "tensor"),
            P("prompt", "tensor"),
            P("prompt", "tensor"),
            P("tensor", "prompt"),
            P("prompt", None, "tensor"),
            P("prompt", None),
            P(("prompt", "tensor"), None),
            P(("prompt", "tensor")),
        ),
        out_specs=P(None, None, ("prompt", "tensor")),
        check_vma=False,
    )
```

```python
import functools
import math

import jax
import jax.numpy as jnp
from jax import lax
from jax.experimental import pallas as pl
from jax.experimental.pallas import tpu as pltpu
from jax.sharding import PartitionSpec as P

KVH = 8
HD = 128


EPSILON = 1e-05


def exchange_kernel(axis, count, spread, *refs):
    arrays = len(spread)
    sources, targets = refs[:arrays], refs[arrays : 2 * arrays]
    send_sem, recv_sem, own_sem = refs[2 * arrays :]
    here = lax.axis_index(axis)

    def block(i, to):
        return sources[i].at[to] if spread[i] else sources[i]

    kept = []
    for i in range(arrays):
        copy = pltpu.make_async_copy(block(i, here), targets[i].at[here], own_sem.at[i])
        copy.start()
        kept.append(copy)
    barrier = pltpu.get_barrier_semaphore()
    for step in range(1, count):
        peer = lax.rem(here + step, count)
        pl.semaphore_signal(
            barrier, inc=1, device_id={axis: peer}, device_id_type=pl.DeviceIdType.MESH
        )
    pl.semaphore_wait(barrier, count - 1)
    copies = []
    for step in range(1, count):
        peer = lax.rem(here + step, count)
        for i in range(arrays):
            copy = pltpu.make_async_remote_copy(
                src_ref=block(i, peer),
                dst_ref=targets[i].at[here],
                send_sem=send_sem.at[i, step - 1],
                recv_sem=recv_sem.at[i, step - 1],
                device_id={axis: peer},
                device_id_type=pl.DeviceIdType.MESH,
            )
            copy.start()
            copies.append(copy)
    for copy in kept + copies:
        copy.wait()


def exchange(axis, number, *operands):
    count = lax.axis_size(axis)
    arrays = [array for array, _ in operands]
    spread = tuple(each for _, each in operands)
    shapes = [
        jax.ShapeDtypeStruct(((count,) + (a.shape[1:] if each else a.shape)), a.dtype)
        for a, each in operands
    ]
    space = pl.BlockSpec(memory_space=pltpu.VMEM)
    sems = pltpu.SemaphoreType.DMA((len(arrays), count - 1))
    return pl.pallas_call(
        functools.partial(exchange_kernel, axis, count, spread),
        out_shape=shapes,
        in_specs=[space] * len(arrays),
        out_specs=[space] * len(arrays),
        scratch_shapes=[sems, sems, pltpu.SemaphoreType.DMA((len(arrays),))],
        compiler_params=pltpu.CompilerParams(
            collective_id=number, has_side_effects=True, vmem_limit_bytes=40 << 20
        ),
    )(*arrays)


def dot_f32(spec, a, b):
    return jnp.einsum(spec, a, b, preferred_element_type=jnp.float32)


MESH = pl.DeviceIdType.MESH


def greet(axis, peers):
    barrier = pltpu.get_barrier_semaphore()
    for peer in peers:
        pl.semaphore_signal(barrier, inc=1, device_id={axis: peer}, device_id_type=MESH)
    pl.semaphore_wait(barrier, len(peers))


def gather_kernel(axis, count, arrays, *refs):
    sources, targets = refs[:arrays], refs[arrays : 2 * arrays]
    send_sem, recv_sem, own_sem = refs[2 * arrays :]
    here = lax.axis_index(axis)
    chips = count // 2
    chip, core = here // 2, lax.rem(here, 2)
    pair = 2 * chip + (1 - core)
    kept = []
    for i in range(arrays):
        copy = pltpu.make_async_copy(sources[i], targets[i].at[here], own_sem.at[i])
        copy.start()
        kept.append(copy)

    def push(i, source, slot, number, peer):
        return pltpu.make_async_remote_copy(
            src_ref=source,
            dst_ref=targets[i].at[slot],
            send_sem=send_sem.at[i, number],
            recv_sem=recv_sem.at[i, number],
            device_id={axis: peer},
            device_id_type=MESH,
        )

    others = [2 * lax.rem(chip + step, chips) + core for step in range(1, chips)]
    greet(axis, others + [pair])
    first = []
    for step in range(1, chips):
        for i in range(arrays):
            copy = push(i, sources[i], here, step, others[step - 1])
            copy.start()
            first.append(copy)
    rest = []
    for i in range(arrays):
        copy = push(i, sources[i], here, 0, pair)
        copy.start()
        rest.append(copy)
    for step in range(1, chips):
        slot = 2 * lax.rem(chip + chips - step, chips) + core
        for i in range(arrays):
            first[(step - 1) * arrays + i].wait_recv()
            copy = push(i, targets[i].at[slot], slot, chips - 1 + step, pair)
            copy.start()
            rest.append(copy)
    for copy in first:
        copy.wait_send()
    for copy in kept + rest:
        copy.wait()


def gather(axis, number, *arrays):
    count = lax.axis_size(axis)
    shapes = [jax.ShapeDtypeStruct((count,) + a.shape, a.dtype) for a in arrays]
    space = pl.BlockSpec(memory_space=pltpu.VMEM)
    sems = pltpu.SemaphoreType.DMA((len(arrays), count - 1))
    return pl.pallas_call(
        functools.partial(gather_kernel, axis, count, len(arrays)),
        out_shape=shapes,
        in_specs=[space] * len(arrays),
        out_specs=[space] * len(arrays),
        scratch_shapes=[sems, sems, pltpu.SemaphoreType.DMA((len(arrays),))],
        compiler_params=pltpu.CompilerParams(
            collective_id=number, has_side_effects=True, vmem_limit_bytes=40 << 20
        ),
    )(*arrays)


def line_kernel(axis, source, target, relay, send_sem, recv_sem, own_sem):
    here = lax.axis_index(axis)
    own = pltpu.make_async_copy(source.at[here], target.at[here], own_sem.at[0])
    own.start()
    greet(axis, [lax.rem(here + step, 4) for step in range(1, 4)])

    def push(block, slot, number, peer, into=None):
        return pltpu.make_async_remote_copy(
            src_ref=block,
            dst_ref=target.at[slot] if into is None else into,
            send_sem=send_sem.at[number],
            recv_sem=recv_sem.at[slot if into is None else 4],
            device_id={axis: peer},
            device_id_type=MESH,
        )

    for role in range(4):
        far = 3 if role < 2 else 0
        middle = 1 if role < 2 else 2
        across = 3 - middle

        @pl.when(here == role)
        def _():
            if role == middle:
                sent = [
                    push(source.at[across], role, 0, across),
                    push(source.at[3 - far], role, 1, 3 - far),
                ]
                for copy in sent:
                    copy.start()
                total = push(relay, role, 2, far)
                push(source.at[far], role, 3, far, relay).wait_recv()
                relay[...] = relay[...] + source[far]
                total.start()
                sent.append(total)
                arriving = [0, across, 3]
            else:
                handed = push(source.at[far], role, 0, middle, relay)
                handed.start()
                target[far] = jnp.zeros_like(target[far])
                handed.wait_send()
                sent = [
                    push(source.at[across], role, 1, across),
                    push(source.at[middle], role, 2, middle),
                ]
                for copy in sent:
                    copy.start()
                arriving = [1, 2]
            for slot in arriving:
                push(source.at[slot], slot, 3, slot).wait_recv()
            for copy in sent:
                copy.wait_send()

    own.wait()


def line_exchange(axis, number, blocks):
    if lax.axis_size(axis) != 4:
        return exchange(axis, number, (blocks, True))[0]
    space = pl.BlockSpec(memory_space=pltpu.VMEM)
    return pl.pallas_call(
        functools.partial(line_kernel, axis),
        out_shape=jax.ShapeDtypeStruct(blocks.shape, blocks.dtype),
        in_specs=[space],
        out_specs=space,
        scratch_shapes=[
            pltpu.VMEM(blocks.shape[1:], blocks.dtype),
            pltpu.SemaphoreType.DMA((4,)),
            pltpu.SemaphoreType.DMA((5,)),
            pltpu.SemaphoreType.DMA((1,)),
        ],
        compiler_params=pltpu.CompilerParams(
            collective_id=number, has_side_effects=True, vmem_limit_bytes=40 << 20
        ),
    )(blocks)


CHUNK = 256


def score_kernel(
    axis, count, part, vocab, scores, got, flat, table, send_sem, recv_sem, own_sem, load_sem
):
    def load(c):
        span = pl.ds(pl.multiple_of(c * CHUNK, CHUNK), CHUNK)
        return pltpu.make_async_copy(vocab.at[span], table.at[span], load_sem.at[c])

    chunks = vocab.shape[0] // CHUNK
    for c in range(chunks):
        load(c).start()
    gather_kernel(axis, count, 1, part, got, send_sem, recv_sem, own_sem)
    wide = part.shape[2]
    for p in range(part.shape[0]):
        for t in range(count):
            start = (p * count + t) * wide
            flat[:, start : start + wide] = got[t, p]

    @pl.loop(0, chunks)
    def _(c):
        load(c).wait()
        span = pl.ds(pl.multiple_of(c * CHUNK, CHUNK), CHUNK)
        scores[:, span] = -lax.dot_general(
            flat[...],
            table[span, :],
            (((1,), (1,)), ((), ())),
            preferred_element_type=jnp.float32,
        )


def gather_score(axis, number, part, vocab):
    count = lax.axis_size(axis)
    n_prompt, rows, wide = part.shape
    vocab_here, width = vocab.shape
    if wide % 128 or vocab_here % CHUNK or rows % 16:
        (part,) = gather(axis, number, part)
        return -dot_f32("rd,vd->rv", part.transpose(2, 1, 0, 3).reshape(rows, width), vocab)
    sems = pltpu.SemaphoreType.DMA((1, count - 1))
    return pl.pallas_call(
        functools.partial(score_kernel, axis, count),
        out_shape=jax.ShapeDtypeStruct((rows, vocab_here), jnp.float32),
        in_specs=[pl.BlockSpec(memory_space=pltpu.VMEM), pl.BlockSpec(memory_space=pl.ANY)],
        out_specs=pl.BlockSpec(memory_space=pltpu.VMEM),
        scratch_shapes=[
            pltpu.VMEM((count,) + part.shape, part.dtype),
            pltpu.VMEM((rows, width), part.dtype),
            pltpu.VMEM(vocab.shape, vocab.dtype),
            sems,
            sems,
            pltpu.SemaphoreType.DMA((1,)),
            pltpu.SemaphoreType.DMA((vocab_here // CHUNK,)),
        ],
        compiler_params=pltpu.CompilerParams(
            collective_id=number, has_side_effects=True, vmem_limit_bytes=52 << 20
        ),
    )(part, vocab)


def on_device(
    embeds,
    norm_gain,
    query_weight,
    key_weight,
    value_weight,
    out_weight,
    out_grad,
    suffix_pos,
    vocab_table,
    banned,
):
    n_prompt = lax.axis_size("prompt")
    n_tensor = lax.axis_size("tensor")
    here_prompt = lax.axis_index("prompt")
    here_tensor = lax.axis_index("tensor")
    seq_len = embeds.shape[1]
    suffix_count = suffix_pos.shape[1]
    width = embeds.shape[2] * n_tensor
    rows_here, head_cols = query_weight.shape
    key_cols = key_weight.shape[1]
    heads_here = head_cols // HD
    slice_width = rows_here // n_tensor
    logit_scale = 1.0 / math.sqrt(HD)

    split_rows = seq_len // n_tensor
    ratio = n_tensor // n_prompt
    feature_cols = embeds.shape[2]
    both = jnp.concatenate(
        [
            embeds.reshape(n_tensor, split_rows, feature_cols),
            out_grad.reshape(n_tensor, split_rows, feature_cols),
        ],
        axis=1,
    )
    (both,) = exchange("tensor", 0, (both, True))
    own = both[:, :split_rows].astype(jnp.float32)
    inverse_norm = lax.rsqrt(jnp.sum(own * own, axis=(0, 2))[:, None] / width + EPSILON)
    inverse_norm = jnp.broadcast_to(inverse_norm, (split_rows, 128))
    both = both.reshape(n_prompt, ratio, 2 * split_rows, feature_cols)
    both, inverse_norm, suffix_all = exchange(
        "prompt", 1, (both, True), (inverse_norm, False), (suffix_pos, False)
    )
    both, inverse_norm = gather("tensor", 2, both, inverse_norm)
    suffix_all = suffix_all.reshape(n_prompt, suffix_count)
    both = both.reshape(n_tensor, n_prompt, ratio, 2, split_rows, feature_cols)
    both = both.transpose(3, 1, 0, 4, 2, 5).reshape(2, n_prompt, seq_len, rows_here)
    embeds, out_grad = both[0], both[1]
    inverse_norm = inverse_norm[..., :1].transpose(1, 0, 2, 3).reshape(n_prompt, seq_len, 1)
    embeds_float = embeds.astype(jnp.float32)
    gain_rows = lax.dynamic_slice_in_dim(norm_gain, here_prompt * rows_here, rows_here, 0)
    gain_rows = gain_rows.astype(jnp.float32)
    normed = (embeds_float * inverse_norm * gain_rows).astype(jnp.bfloat16)

    parts = jnp.concatenate(
        [
            dot_f32("psd,dc->psc", normed, query_weight),
            dot_f32("psd,dc->psc", normed, key_weight),
            dot_f32("psd,dc->psc", normed, value_weight),
            dot_f32("psd,cd->psc", out_grad, out_weight),
        ],
        axis=2,
    )
    parts = line_exchange("prompt", 3, parts)
    whole = jnp.sum(parts, axis=0).astype(jnp.bfloat16)
    contexts = whole[:, head_cols + 2 * key_cols :]
    contexts = contexts.reshape(seq_len, heads_here, HD)
    queries = whole[:, :head_cols].reshape(seq_len, heads_here, HD)
    (key_values,) = gather("tensor", 4, whole[:, head_cols : head_cols + 2 * key_cols])
    key_values = key_values.reshape(n_tensor, seq_len, 2, key_cols).transpose(2, 1, 0, 3)
    key_values = key_values.reshape(2, seq_len, KVH * HD)
    fold = min(heads_here, KVH)
    first = ((here_tensor * heads_here) % KVH) * HD
    if fold < KVH:
        key_values = lax.dynamic_slice_in_dim(key_values, first, fold * HD, 2)
    key_values = key_values.reshape(2, seq_len, fold, HD)
    if heads_here > fold:
        key_values = jnp.tile(key_values, (1, 1, heads_here // fold, 1))
    keys, values = key_values[0], key_values[1]

    logits = dot_f32("qhd,khd->hqk", queries, keys) * logit_scale
    row_index = lax.broadcasted_iota(jnp.int32, (seq_len, seq_len), 0)
    col_index = lax.broadcasted_iota(jnp.int32, (seq_len, seq_len), 1)
    causal = col_index <= row_index
    largest = jnp.max(jnp.where(causal, logits, -1e30), axis=-1, keepdims=True)
    raised = jnp.where(causal, jnp.exp(logits - largest), 0.0)
    probs = raised / jnp.sum(raised, axis=-1, keepdims=True)
    probs_low = probs.astype(jnp.bfloat16)
    prob_grad = dot_f32("qhd,khd->hqk", contexts, values)
    logit_grad = (
        probs * (prob_grad - jnp.sum(prob_grad * probs, axis=-1, keepdims=True)) * logit_scale
    ).astype(jnp.bfloat16)
    steps_iota = lax.broadcasted_iota(jnp.int32, (suffix_count, seq_len), 1)
    chooser = (steps_iota == suffix_pos[0][:, None]).astype(jnp.bfloat16)
    logit_rows = dot_f32("ns,hsk->hnk", chooser, logit_grad).astype(jnp.bfloat16)
    query_grad = dot_f32("hnk,khd->nhd", logit_rows, keys).astype(jnp.bfloat16)
    query_grad = query_grad.reshape(suffix_count, head_cols)
    logit_cols = dot_f32("hqk,nk->hnq", logit_grad, chooser).astype(jnp.bfloat16)
    prob_cols = dot_f32("hqk,nk->hnq", probs_low, chooser).astype(jnp.bfloat16)
    key_each = dot_f32("hnq,qhd->nhd", logit_cols, queries)
    value_each = dot_f32("hnq,qhd->nhd", prob_cols, contexts)
    slots = jnp.stack([key_each, value_each])
    slots = slots.reshape(2, suffix_count, heads_here // fold, fold * HD).sum(axis=2)
    if fold < KVH:
        slots = lax.dynamic_update_slice_in_dim(
            jnp.zeros((2, suffix_count, KVH * HD), jnp.float32), slots, first, 2
        )
    slots = slots.reshape(2 * suffix_count, n_tensor, key_cols).transpose(1, 0, 2)
    (grads,) = exchange("tensor", 5, (slots, True))
    grads = jnp.sum(grads, axis=0).astype(jnp.bfloat16).reshape(2, suffix_count, key_cols)
    grads = jnp.concatenate([query_grad, grads[0], grads[1]], axis=1)
    (grads,) = exchange("prompt", 6, (grads, False))
    rows = n_prompt * suffix_count
    grads = grads.reshape(rows, head_cols + 2 * key_cols)
    steps_iota = lax.broadcasted_iota(jnp.int32, (n_prompt, suffix_count, seq_len), 2)
    chooser_all = steps_iota == suffix_all[:, :, None]
    embed_rows = dot_f32("pns,psd->pnd", chooser_all.astype(jnp.bfloat16), embeds)
    norm_rows = jnp.sum(
        jnp.where(chooser_all, inverse_norm[:, None, :, 0], 0.0), axis=-1, keepdims=True
    )
    scaled = (embed_rows * norm_rows).reshape(rows, rows_here)
    norm_rows = norm_rows.reshape(rows, 1)
    branch = dot_f32("nc,dc->nd", grads[:, :head_cols], query_weight)
    branch = branch + dot_f32("nc,dc->nd", grads[:, head_cols : head_cols + key_cols], key_weight)
    branch = branch + dot_f32("nc,dc->nd", grads[:, head_cols + key_cols :], value_weight)
    branch = branch * gain_rows
    inner = jnp.sum(branch * scaled, axis=-1)
    branch = branch.reshape(rows, n_tensor, slice_width).transpose(1, 0, 2)
    share, inner = exchange("tensor", 7, (branch, True), (inner[None, :], False))
    weighted = jnp.sum(share, axis=0)
    (inner,) = exchange("prompt", 8, (jnp.sum(inner, axis=0), False))
    inner = jnp.sum(inner, axis=0).reshape(rows, 1) / width
    scaled = lax.dynamic_slice_in_dim(scaled, here_tensor * slice_width, slice_width, 1)
    suffix_grad = (norm_rows * (weighted - scaled * inner)).astype(jnp.bfloat16)
    (suffix_grad,) = exchange("prompt", 9, (suffix_grad, False))
    scores = gather_score("tensor", 10, suffix_grad, vocab_table)
    scores = scores.reshape(n_prompt, suffix_count, vocab_table.shape[0])
    return jnp.where(banned[None, None, :] == 1, 0.0, scores)


def solution(mesh):
    return jax.shard_map(
        on_device,
        mesh=mesh,
        in_specs=(
            P("prompt", None, "tensor"),
            P(),
            P("prompt", "tensor"),
            P("prompt", "tensor"),
            P("prompt", "tensor"),
            P("tensor", "prompt"),
            P("prompt", None, "tensor"),
            P("prompt", None),
            P(("prompt", "tensor"), None),
            P(("prompt", "tensor")),
        ),
        out_specs=P(None, None, ("prompt", "tensor")),
        check_vma=False,
    )
```

```python
import functools
import math

import jax
import jax.numpy as jnp
from jax import lax
from jax.experimental import pallas as pl
from jax.experimental.pallas import tpu as pltpu
from jax.sharding import PartitionSpec as P

KVH = 8
HD = 128


EPSILON = 1e-05


def exchange_kernel(axis, count, spread, *refs):
    arrays = len(spread)
    sources, targets = refs[:arrays], refs[arrays : 2 * arrays]
    send_sem, recv_sem, own_sem = refs[2 * arrays :]
    here = lax.axis_index(axis)

    def block(i, to):
        return sources[i].at[to] if spread[i] else sources[i]

    kept = []
    for i in range(arrays):
        copy = pltpu.make_async_copy(block(i, here), targets[i].at[here], own_sem.at[i])
        copy.start()
        kept.append(copy)
    barrier = pltpu.get_barrier_semaphore()
    for step in range(1, count):
        peer = lax.rem(here + step, count)
        pl.semaphore_signal(
            barrier, inc=1, device_id={axis: peer}, device_id_type=pl.DeviceIdType.MESH
        )
    pl.semaphore_wait(barrier, count - 1)
    copies = []
    for step in range(1, count):
        peer = lax.rem(here + step, count)
        for i in range(arrays):
            copy = pltpu.make_async_remote_copy(
                src_ref=block(i, peer),
                dst_ref=targets[i].at[here],
                send_sem=send_sem.at[i, step - 1],
                recv_sem=recv_sem.at[i, step - 1],
                device_id={axis: peer},
                device_id_type=pl.DeviceIdType.MESH,
            )
            copy.start()
            copies.append(copy)
    for copy in kept + copies:
        copy.wait()


def exchange(axis, number, *operands):
    count = lax.axis_size(axis)
    arrays = [array for array, _ in operands]
    spread = tuple(each for _, each in operands)
    shapes = [
        jax.ShapeDtypeStruct(((count,) + (a.shape[1:] if each else a.shape)), a.dtype)
        for a, each in operands
    ]
    space = pl.BlockSpec(memory_space=pltpu.VMEM)
    sems = pltpu.SemaphoreType.DMA((len(arrays), count - 1))
    return pl.pallas_call(
        functools.partial(exchange_kernel, axis, count, spread),
        out_shape=shapes,
        in_specs=[space] * len(arrays),
        out_specs=[space] * len(arrays),
        scratch_shapes=[sems, sems, pltpu.SemaphoreType.DMA((len(arrays),))],
        compiler_params=pltpu.CompilerParams(
            collective_id=number, has_side_effects=True, vmem_limit_bytes=40 << 20
        ),
    )(*arrays)


def dot_f32(spec, a, b):
    return jnp.einsum(spec, a, b, preferred_element_type=jnp.float32)


MESH = pl.DeviceIdType.MESH


def greet(axis, peers):
    barrier = pltpu.get_barrier_semaphore()
    for peer in peers:
        pl.semaphore_signal(barrier, inc=1, device_id={axis: peer}, device_id_type=MESH)
    pl.semaphore_wait(barrier, len(peers))


def gather_kernel(axis, count, arrays, *refs):
    sources, targets = refs[:arrays], refs[arrays : 2 * arrays]
    send_sem, recv_sem, own_sem = refs[2 * arrays :]
    here = lax.axis_index(axis)
    chips = count // 2
    chip, core = here // 2, lax.rem(here, 2)
    pair = 2 * chip + (1 - core)
    kept = []
    for i in range(arrays):
        copy = pltpu.make_async_copy(sources[i], targets[i].at[here], own_sem.at[i])
        copy.start()
        kept.append(copy)

    def push(i, source, slot, number, peer):
        return pltpu.make_async_remote_copy(
            src_ref=source,
            dst_ref=targets[i].at[slot],
            send_sem=send_sem.at[i, number],
            recv_sem=recv_sem.at[i, number],
            device_id={axis: peer},
            device_id_type=MESH,
        )

    others = [2 * lax.rem(chip + step, chips) + core for step in range(1, chips)]
    greet(axis, others + [pair])
    first = []
    for step in range(1, chips):
        for i in range(arrays):
            copy = push(i, sources[i], here, step, others[step - 1])
            copy.start()
            first.append(copy)
    rest = []
    for i in range(arrays):
        copy = push(i, sources[i], here, 0, pair)
        copy.start()
        rest.append(copy)
    for step in range(1, chips):
        slot = 2 * lax.rem(chip + chips - step, chips) + core
        for i in range(arrays):
            first[(step - 1) * arrays + i].wait_recv()
            copy = push(i, targets[i].at[slot], slot, chips - 1 + step, pair)
            copy.start()
            rest.append(copy)
    for copy in first:
        copy.wait_send()
    for copy in kept + rest:
        copy.wait()


def gather(axis, number, *arrays):
    count = lax.axis_size(axis)
    shapes = [jax.ShapeDtypeStruct((count,) + a.shape, a.dtype) for a in arrays]
    space = pl.BlockSpec(memory_space=pltpu.VMEM)
    sems = pltpu.SemaphoreType.DMA((len(arrays), count - 1))
    return pl.pallas_call(
        functools.partial(gather_kernel, axis, count, len(arrays)),
        out_shape=shapes,
        in_specs=[space] * len(arrays),
        out_specs=[space] * len(arrays),
        scratch_shapes=[sems, sems, pltpu.SemaphoreType.DMA((len(arrays),))],
        compiler_params=pltpu.CompilerParams(
            collective_id=number, has_side_effects=True, vmem_limit_bytes=40 << 20
        ),
    )(*arrays)


def line_kernel(axis, source, target, relay, send_sem, recv_sem, own_sem):
    here = lax.axis_index(axis)
    own = pltpu.make_async_copy(source.at[here], target.at[here], own_sem.at[0])
    own.start()
    greet(axis, [lax.rem(here + step, 4) for step in range(1, 4)])

    def push(block, slot, number, peer, into=None):
        return pltpu.make_async_remote_copy(
            src_ref=block,
            dst_ref=target.at[slot] if into is None else into,
            send_sem=send_sem.at[number],
            recv_sem=recv_sem.at[slot if into is None else 4],
            device_id={axis: peer},
            device_id_type=MESH,
        )

    for role in range(4):
        far = 3 if role < 2 else 0
        middle = 1 if role < 2 else 2
        across = 3 - middle

        @pl.when(here == role)
        def _():
            if role == middle:
                sent = [
                    push(source.at[across], role, 0, across),
                    push(source.at[3 - far], role, 1, 3 - far),
                ]
                for copy in sent:
                    copy.start()
                total = push(relay, role, 2, far)
                push(source.at[far], role, 3, far, relay).wait_recv()
                relay[...] = relay[...] + source[far]
                total.start()
                sent.append(total)
                arriving = [0, across, 3]
            else:
                handed = push(source.at[far], role, 0, middle, relay)
                handed.start()
                target[far] = jnp.zeros_like(target[far])
                handed.wait_send()
                sent = [
                    push(source.at[across], role, 1, across),
                    push(source.at[middle], role, 2, middle),
                ]
                for copy in sent:
                    copy.start()
                arriving = [1, 2]
            for slot in arriving:
                push(source.at[slot], slot, 3, slot).wait_recv()
            for copy in sent:
                copy.wait_send()

    own.wait()


def line_exchange(axis, number, blocks):
    if lax.axis_size(axis) != 4:
        return exchange(axis, number, (blocks, True))[0]
    space = pl.BlockSpec(memory_space=pltpu.VMEM)
    return pl.pallas_call(
        functools.partial(line_kernel, axis),
        out_shape=jax.ShapeDtypeStruct(blocks.shape, blocks.dtype),
        in_specs=[space],
        out_specs=space,
        scratch_shapes=[
            pltpu.VMEM(blocks.shape[1:], blocks.dtype),
            pltpu.SemaphoreType.DMA((4,)),
            pltpu.SemaphoreType.DMA((5,)),
            pltpu.SemaphoreType.DMA((1,)),
        ],
        compiler_params=pltpu.CompilerParams(
            collective_id=number, has_side_effects=True, vmem_limit_bytes=40 << 20
        ),
    )(blocks)


CHUNK = 512


def score_kernel(
    axis, count, part, vocab, scores, got, flat, table, send_sem, recv_sem, own_sem, load_sem
):
    def load(c):
        span = pl.ds(pl.multiple_of(c * CHUNK, CHUNK), CHUNK)
        return pltpu.make_async_copy(vocab.at[span], table.at[span], load_sem.at[c])

    chunks = vocab.shape[0] // CHUNK
    for c in range(chunks):
        load(c).start()
    gather_kernel(axis, count, 1, part, got, send_sem, recv_sem, own_sem)
    wide = part.shape[2]
    for p in range(part.shape[0]):
        for t in range(count):
            start = (p * count + t) * wide
            flat[:, start : start + wide] = got[t, p]

    @pl.loop(0, chunks)
    def _(c):
        load(c).wait()
        span = pl.ds(pl.multiple_of(c * CHUNK, CHUNK), CHUNK)
        scores[:, span] = -lax.dot_general(
            flat[...],
            table[span, :],
            (((1,), (1,)), ((), ())),
            preferred_element_type=jnp.float32,
        )


def gather_score(axis, number, part, vocab):
    count = lax.axis_size(axis)
    n_prompt, rows, wide = part.shape
    vocab_here, width = vocab.shape
    if wide % 128 or vocab_here % CHUNK or rows % 16:
        (part,) = gather(axis, number, part)
        return -dot_f32("rd,vd->rv", part.transpose(2, 1, 0, 3).reshape(rows, width), vocab)
    sems = pltpu.SemaphoreType.DMA((1, count - 1))
    return pl.pallas_call(
        functools.partial(score_kernel, axis, count),
        out_shape=jax.ShapeDtypeStruct((rows, vocab_here), jnp.float32),
        in_specs=[pl.BlockSpec(memory_space=pltpu.VMEM), pl.BlockSpec(memory_space=pl.ANY)],
        out_specs=pl.BlockSpec(memory_space=pltpu.VMEM),
        scratch_shapes=[
            pltpu.VMEM((count,) + part.shape, part.dtype),
            pltpu.VMEM((rows, width), part.dtype),
            pltpu.VMEM(vocab.shape, vocab.dtype),
            sems,
            sems,
            pltpu.SemaphoreType.DMA((1,)),
            pltpu.SemaphoreType.DMA((vocab_here // CHUNK,)),
        ],
        compiler_params=pltpu.CompilerParams(
            collective_id=number, has_side_effects=True, vmem_limit_bytes=52 << 20
        ),
    )(part, vocab)


def on_device(
    embeds,
    norm_gain,
    query_weight,
    key_weight,
    value_weight,
    out_weight,
    out_grad,
    suffix_pos,
    vocab_table,
    banned,
):
    n_prompt = lax.axis_size("prompt")
    n_tensor = lax.axis_size("tensor")
    here_prompt = lax.axis_index("prompt")
    here_tensor = lax.axis_index("tensor")
    seq_len = embeds.shape[1]
    suffix_count = suffix_pos.shape[1]
    width = embeds.shape[2] * n_tensor
    rows_here, head_cols = query_weight.shape
    key_cols = key_weight.shape[1]
    heads_here = head_cols // HD
    slice_width = rows_here // n_tensor
    logit_scale = 1.0 / math.sqrt(HD)

    split_rows = seq_len // n_tensor
    ratio = n_tensor // n_prompt
    feature_cols = embeds.shape[2]
    both = jnp.concatenate(
        [
            embeds.reshape(n_tensor, split_rows, feature_cols),
            out_grad.reshape(n_tensor, split_rows, feature_cols),
        ],
        axis=1,
    )
    (both,) = exchange("tensor", 0, (both, True))
    own = both[:, :split_rows].astype(jnp.float32)
    inverse_norm = lax.rsqrt(jnp.sum(own * own, axis=(0, 2))[:, None] / width + EPSILON)
    inverse_norm = jnp.broadcast_to(inverse_norm, (split_rows, 128))
    both = both.reshape(n_prompt, ratio, 2 * split_rows, feature_cols)
    both, inverse_norm, suffix_all = exchange(
        "prompt", 1, (both, True), (inverse_norm, False), (suffix_pos, False)
    )
    both, inverse_norm = gather("tensor", 2, both, inverse_norm)
    suffix_all = suffix_all.reshape(n_prompt, suffix_count)
    both = both.reshape(n_tensor, n_prompt, ratio, 2, split_rows, feature_cols)
    both = both.transpose(3, 1, 0, 4, 2, 5).reshape(2, n_prompt, seq_len, rows_here)
    embeds, out_grad = both[0], both[1]
    inverse_norm = inverse_norm[..., :1].transpose(1, 0, 2, 3).reshape(n_prompt, seq_len, 1)
    embeds_float = embeds.astype(jnp.float32)
    gain_rows = lax.dynamic_slice_in_dim(norm_gain, here_prompt * rows_here, rows_here, 0)
    gain_rows = gain_rows.astype(jnp.float32)
    normed = (embeds_float * inverse_norm * gain_rows).astype(jnp.bfloat16)

    parts = jnp.concatenate(
        [
            dot_f32("psd,dc->psc", normed, query_weight),
            dot_f32("psd,dc->psc", normed, key_weight),
            dot_f32("psd,dc->psc", normed, value_weight),
            dot_f32("psd,cd->psc", out_grad, out_weight),
        ],
        axis=2,
    )
    parts = line_exchange("prompt", 3, parts)
    whole = jnp.sum(parts, axis=0).astype(jnp.bfloat16)
    contexts = whole[:, head_cols + 2 * key_cols :]
    contexts = contexts.reshape(seq_len, heads_here, HD)
    queries = whole[:, :head_cols].reshape(seq_len, heads_here, HD)
    (key_values,) = gather("tensor", 4, whole[:, head_cols : head_cols + 2 * key_cols])
    key_values = key_values.reshape(n_tensor, seq_len, 2, key_cols).transpose(2, 1, 0, 3)
    key_values = key_values.reshape(2, seq_len, KVH * HD)
    fold = min(heads_here, KVH)
    first = ((here_tensor * heads_here) % KVH) * HD
    if fold < KVH:
        key_values = lax.dynamic_slice_in_dim(key_values, first, fold * HD, 2)
    key_values = key_values.reshape(2, seq_len, fold, HD)
    if heads_here > fold:
        key_values = jnp.tile(key_values, (1, 1, heads_here // fold, 1))
    keys, values = key_values[0], key_values[1]

    logits = dot_f32("qhd,khd->hqk", queries, keys) * logit_scale
    row_index = lax.broadcasted_iota(jnp.int32, (seq_len, seq_len), 0)
    col_index = lax.broadcasted_iota(jnp.int32, (seq_len, seq_len), 1)
    causal = col_index <= row_index
    largest = jnp.max(jnp.where(causal, logits, -1e30), axis=-1, keepdims=True)
    raised = jnp.where(causal, jnp.exp(logits - largest), 0.0)
    probs = raised / jnp.sum(raised, axis=-1, keepdims=True)
    probs_low = probs.astype(jnp.bfloat16)
    prob_grad = dot_f32("qhd,khd->hqk", contexts, values)
    logit_grad = (
        probs * (prob_grad - jnp.sum(prob_grad * probs, axis=-1, keepdims=True)) * logit_scale
    ).astype(jnp.bfloat16)
    steps_iota = lax.broadcasted_iota(jnp.int32, (suffix_count, seq_len), 1)
    chooser = (steps_iota == suffix_pos[0][:, None]).astype(jnp.bfloat16)
    logit_rows = dot_f32("ns,hsk->hnk", chooser, logit_grad).astype(jnp.bfloat16)
    query_grad = dot_f32("hnk,khd->nhd", logit_rows, keys).astype(jnp.bfloat16)
    query_grad = query_grad.reshape(suffix_count, head_cols)
    logit_cols = dot_f32("hqk,nk->hnq", logit_grad, chooser).astype(jnp.bfloat16)
    prob_cols = dot_f32("hqk,nk->hnq", probs_low, chooser).astype(jnp.bfloat16)
    key_each = dot_f32("hnq,qhd->nhd", logit_cols, queries)
    value_each = dot_f32("hnq,qhd->nhd", prob_cols, contexts)
    slots = jnp.stack([key_each, value_each])
    slots = slots.reshape(2, suffix_count, heads_here // fold, fold * HD).sum(axis=2)
    if fold < KVH:
        slots = lax.dynamic_update_slice_in_dim(
            jnp.zeros((2, suffix_count, KVH * HD), jnp.float32), slots, first, 2
        )
    slots = slots.reshape(2 * suffix_count, n_tensor, key_cols).transpose(1, 0, 2)
    (grads,) = exchange("tensor", 5, (slots, True))
    grads = jnp.sum(grads, axis=0).astype(jnp.bfloat16).reshape(2, suffix_count, key_cols)
    grads = jnp.concatenate([query_grad, grads[0], grads[1]], axis=1)
    (grads,) = exchange("prompt", 6, (grads, False))
    rows = n_prompt * suffix_count
    grads = grads.reshape(rows, head_cols + 2 * key_cols)
    steps_iota = lax.broadcasted_iota(jnp.int32, (n_prompt, suffix_count, seq_len), 2)
    chooser_all = steps_iota == suffix_all[:, :, None]
    embed_rows = dot_f32("pns,psd->pnd", chooser_all.astype(jnp.bfloat16), embeds)
    norm_rows = jnp.sum(
        jnp.where(chooser_all, inverse_norm[:, None, :, 0], 0.0), axis=-1, keepdims=True
    )
    scaled = (embed_rows * norm_rows).reshape(rows, rows_here)
    norm_rows = norm_rows.reshape(rows, 1)
    branch = dot_f32("nc,dc->nd", grads[:, :head_cols], query_weight)
    branch = branch + dot_f32("nc,dc->nd", grads[:, head_cols : head_cols + key_cols], key_weight)
    branch = branch + dot_f32("nc,dc->nd", grads[:, head_cols + key_cols :], value_weight)
    branch = branch * gain_rows
    inner = jnp.sum(branch * scaled, axis=-1)
    branch = branch.reshape(rows, n_tensor, slice_width).transpose(1, 0, 2)
    share, inner = exchange("tensor", 7, (branch, True), (inner[None, :], False))
    weighted = jnp.sum(share, axis=0)
    (inner,) = exchange("prompt", 8, (jnp.sum(inner, axis=0), False))
    inner = jnp.sum(inner, axis=0).reshape(rows, 1) / width
    scaled = lax.dynamic_slice_in_dim(scaled, here_tensor * slice_width, slice_width, 1)
    suffix_grad = (norm_rows * (weighted - scaled * inner)).astype(jnp.bfloat16)
    (suffix_grad,) = exchange("prompt", 9, (suffix_grad, False))
    scores = gather_score("tensor", 10, suffix_grad, vocab_table)
    scores = scores.reshape(n_prompt, suffix_count, vocab_table.shape[0])
    return jnp.where(banned[None, None, :] == 1, 0.0, scores)


def solution(mesh):
    return jax.shard_map(
        on_device,
        mesh=mesh,
        in_specs=(
            P("prompt", None, "tensor"),
            P(),
            P("prompt", "tensor"),
            P("prompt", "tensor"),
            P("prompt", "tensor"),
            P("tensor", "prompt"),
            P("prompt", None, "tensor"),
            P("prompt", None),
            P(("prompt", "tensor"), None),
            P(("prompt", "tensor")),
        ),
        out_specs=P(None, None, ("prompt", "tensor")),
        check_vma=False,
    )
```
